768 devices in a mesh: dom: 192 (over y, z, core), sub: 4 (over x).
Axes of the slice: x: 4, y: 8, z: 12, core: 2. Of those that a mesh axis runs over, the one named last changes fastest.
Arguments:
- modal_state: float32 [35, 9, 98304], P(None, None, ('dom', 'sub')), may hold values from -6 to 6
- star_matrices: float32 [3, 9, 9, 98304], P(None, None, None, ('dom', 'sub')), may hold values from -2 to 2
- face_normals: float32 [3, 4, 98304], P(None, None, ('dom', 'sub')), may hold values from -4 to 4
- wave_speed: float32 [98304], P(('dom', 'sub')), may hold values from 1 to 3
- inverse_jacobian: float32 [98304], P(('dom', 'sub')), may hold values from 0.02 to 0.2
- stiffness: float32 [3, 35, 35], replicated, may hold values from -1 to 1
- lift_minus: float32 [4, 35, 35], replicated, may hold values from -1 to 1
- lift_plus: float32 [4, 35, 35], replicated, may hold values from -1 to 1
- cluster: int32 [98304], P(('dom', 'sub')), may hold values from 0 to 1, as said below
- face_source: int32 [4, 98304], P(None, ('dom', 'sub')), may hold values from 0 to 207, as said below
- send_rows: int32 [768, 2, 5, 4, 4], P(('dom', 'sub')), may hold values from 0 to 127
- send_counts: int32 [768, 2, 5, 4], P(('dom', 'sub')), may hold values from 0 to 4, as said below
Outputs:
- new_state: float32 [35, 9, 98304], P(None, None, ('dom', 'sub'))
The draws below stay inside these ranges and needn't reach their ends.
Inputs may be any that keep to these rules, and one draw needn't show every extreme that they name: At most 16 elements of one device have cluster 0, and some device has exactly 16. `face_source`: values below 128 name a local element; a larger value names a row of the receive pool of the element's own cluster list. `send_counts`: zero for a device's own slot (offset 2, its own sub index) and for targets beyond the ends of dom; some count equals 4.
All inputs are finite; a program needn't handle non-finite values.
Results may differ from the reference program's by a relative error of at most 0.0003.
Values sent between devices are 32-bit elements; how exact they have to be, the bound alone decides.
No kernel may reach another device: no remote copies, remote signals or barrier semaphores. Data moves between devices by JAX's collectives and lax.ppermute only.
A program may use at most 64 MiB of HBM per device.

```python
import math
import jax
import jax.numpy as jnp
from jax import lax

BASIS = 35
QUANTS = 9
DEGREE = 4
SPAN = 2
ELEM_DEV = 128
FINE_CAP = 16
SLOT_CAP = 4
ELEMENTS = 98304
OFFSETS = 5
POOL = 80
N_DOM = 192
N_SUB = 4


def draw_cluster(key, part):
    count_key, choose_key, order_key = jax.random.split(key, 3)
    device_total = N_DOM * N_SUB
    base_draw = jax.random.randint(count_key, (device_total,), 1, FINE_CAP + 1)
    fine_counts = base_draw * base_draw // FINE_CAP
    chosen = jax.random.randint(choose_key, (), 0, device_total)
    fine_counts = jnp.where(jnp.arange(device_total) == chosen, FINE_CAP, fine_counts)
    ordering = jax.vmap(lambda sub_key: jax.random.permutation(sub_key, ELEM_DEV))(jax.random.split(order_key, device_total))
    is_fine = ordering < fine_counts[:, None]
    return jnp.where(is_fine, 0, 1).astype(jnp.int32).reshape(-1)


def draw_face_source(key, part):
    kind_key, local_key, remote_key = jax.random.split(key, 3)
    layout = (4, ELEMENTS)
    remote = jax.random.randint(kind_key, layout, 0, 8) < 3
    local_rows = jax.random.randint(local_key, layout, 0, ELEM_DEV)
    pool_rows = ELEM_DEV + jax.random.randint(remote_key, layout, 0, POOL)
    picked = jnp.where(remote, pool_rows, local_rows)
    picked = picked.at[0, 0].set(ELEM_DEV + POOL - 1).at[1, 0].set(0)
    return picked.astype(jnp.int32)


def draw_send_counts(key, part):
    amount_key, link_key = jax.random.split(key)
    layout = (N_DOM * N_SUB, 2, 2 * SPAN + 1, N_SUB)
    amounts = jax.random.randint(amount_key, layout, SLOT_CAP // 2, SLOT_CAP + 1)
    linked = jax.random.randint(link_key, layout, 0, 4) > 0
    device = lax.broadcasted_iota(jnp.int32, layout, 0)
    offset = lax.broadcasted_iota(jnp.int32, layout, 2) - SPAN
    target = lax.broadcasted_iota(jnp.int32, layout, 3)
    dom_target = device // N_SUB + offset
    allowed = (dom_target >= 0) & (dom_target < N_DOM) & ((offset != 0) | (target != device % N_SUB))
    amounts = jnp.where(linked & allowed, amounts, 0)
    amounts = amounts.at[0, 0, SPAN + 1, 0].set(SLOT_CAP)
    return amounts.astype(jnp.int32)


def with_ends(values, rng, least, top_value):
    dims = values.shape
    spot = [jax.random.randint(jax.random.fold_in(rng, axis), (), 0, dims[axis]) for axis in range(len(dims))]
    values = values.at[tuple(spot)].set(least)
    longest = dims.index(max(dims))
    spot[longest] = (spot[longest] + 1) % dims[longest]
    return values.at[tuple(spot)].set(top_value)


def block_levels(own_key, dims, cuts, least, top_value):
    loudness, own = 1.0, jax.random.fold_in(own_key, 6)
    for position, parts in cuts:
        draws = jnp.exp(jax.random.uniform(jax.random.fold_in(own, position), (parts,), jnp.float32, least / len(cuts), top_value / len(cuts)))
        loudness = loudness * jnp.repeat(draws, dims[position] // parts).reshape([-1 if axis == position else 1 for axis in range(len(dims))])
    return loudness


def centred(rng, shape, width, bound, pieces=(), kind=jnp.bfloat16):
    result = jax.random.normal(rng, shape, jnp.float32) * width
    if len(pieces) > 0:
        result = block_levels(rng, shape, pieces, -0.22, 0.18) * result
    return jnp.clip(result, min=-bound, max=bound).astype(kind)


def setup_inputs(seed: int = 0) -> dict:
    seeds = jax.random.split(jax.random.key(seed), 13)
    modal_state = centred(seeds[0], (BASIS, QUANTS, ELEMENTS), 1.0, 6.0, ((2, 768),), jnp.float32)
    star_matrices = centred(seeds[1], (3, QUANTS, QUANTS, ELEMENTS), QUANTS ** -0.5, 2.0, ((3, 768),), jnp.float32)
    face_normals = centred(seeds[2], (3, 4, ELEMENTS), 1.0, 4.0, ((2, 768),), jnp.float32)
    wave_speed = jnp.clip(jnp.exp(math.log(3.0) - 1.0986123 * jax.random.uniform(seeds[3], (ELEMENTS,), jnp.float32) ** block_levels(seeds[3], (ELEMENTS,), ((0, 768),), -0.2, 0.2)), 1.0, 3.0)
    inverse_jacobian = jnp.clip(jnp.exp(math.log(0.2) - 2.3025851 * jax.random.uniform(seeds[4], (ELEMENTS,), jnp.float32) ** block_levels(seeds[4], (ELEMENTS,), ((0, 768),), -0.2, 0.2)), 0.02, 0.2)
    stiffness = centred(seeds[5], (3, BASIS, BASIS), BASIS ** -0.5, 1.0, (), jnp.float32)
    lift_minus = centred(seeds[6], (4, BASIS, BASIS), BASIS ** -0.5, 1.0, (), jnp.float32)
    lift_plus = centred(seeds[7], (4, BASIS, BASIS), BASIS ** -0.5, 1.0, (), jnp.float32)
    cluster = draw_cluster(jax.random.fold_in(seeds[12], 71), 0)
    face_source = draw_face_source(jax.random.fold_in(seeds[12], 71), 0)
    send_rows = with_ends(jax.random.randint(seeds[10], (N_DOM * N_SUB, 2, OFFSETS, N_SUB, SLOT_CAP), 0, ELEM_DEV), jax.random.fold_in(seeds[10], 1), 0, ELEM_DEV - 1).astype(jnp.int32)
    send_counts = draw_send_counts(jax.random.fold_in(seeds[12], 71), 0)
    return {"modal_state": modal_state, "star_matrices": star_matrices, "face_normals": face_normals, "wave_speed": wave_speed, "inverse_jacobian": inverse_jacobian, "stiffness": stiffness, "lift_minus": lift_minus, "lift_plus": lift_plus, "cluster": cluster, "face_source": face_source, "send_rows": send_rows, "send_counts": send_counts}


half_step = 0.5
top_precision = lax.Precision.HIGHEST


def quantity_mix(values, matrices):
    total = values[:, 0:1, :] * matrices[0][None]
    for inner in range(1, values.shape[1]):
        total = total + values[:, inner:inner + 1, :] * matrices[inner][None]
    return total


def basis_mix(matrix, values):
    return jnp.einsum("cb,bqe->cqe", matrix, values, precision=top_precision)


def basis_mix_back(matrix, values):
    return jnp.einsum("bc,bqe->cqe", matrix, values, precision=top_precision)


def derivative(values, star_local, stiffness):
    summed = basis_mix(stiffness[0], quantity_mix(values, star_local[0]))
    for direction in range(1, 3):
        summed = summed + basis_mix(stiffness[direction], quantity_mix(values, star_local[direction]))
    return -summed


def integrals(values, star_local, stiffness, intervals):
    results = [(upper_time - lower_time) * values for lower_time, upper_time in intervals]
    current = values
    for degree_now in range(1, DEGREE + 1):
        current = derivative(current, star_local, stiffness)
        factor = float(math.factorial(degree_now + 1))
        results = [acc_value + ((upper_time ** (degree_now + 1) - lower_time ** (degree_now + 1)) / factor) * current for acc_value, (lower_time, upper_time) in zip(results, intervals)]
    return results


def update(integral, sources, star_local, normal_local, speed_local, stiffness, lift_minus, lift_plus):
    summed = basis_mix_back(stiffness[0], quantity_mix(integral, star_local[0]))
    for direction in range(1, 3):
        summed = summed + basis_mix_back(stiffness[direction], quantity_mix(integral, star_local[direction]))
    for face_index in range(4):
        normal_mats = normal_local[0, face_index][None, None, :] * star_local[0]
        for direction in range(1, 3):
            normal_mats = normal_mats + normal_local[direction, face_index][None, None, :] * star_local[direction]
        inner_flux = 0.5 * quantity_mix(integral, normal_mats) + 0.5 * speed_local * integral
        outer_flux = 0.5 * quantity_mix(sources[face_index], normal_mats) - 0.5 * speed_local * sources[face_index]
        summed = summed - basis_mix(lift_minus[face_index], inner_flux) - basis_mix(lift_plus[face_index], outer_flux)
    return summed


def neighbours(local_values, pool_rows, face_rows):
    joined = jnp.concatenate([local_values, pool_rows], axis=2)
    return [jnp.take(joined, face_rows[face_index], axis=2) for face_index in range(4)]


def outgoing(values, slot_rows, slot_counts):
    picked = jnp.take(values, slot_rows.reshape(-1), axis=2)
    picked = picked.reshape((values.shape[0], values.shape[1]) + slot_rows.shape)
    live_slots = lax.broadcasted_iota(jnp.int32, slot_rows.shape, 2) < slot_counts[:, :, None]
    return jnp.where(live_slots[None, None], picked, jnp.zeros_like(picked))


def pull(blocks, device):
    dom_index = device // N_SUB
    sub_index = device % N_SUB
    offset_ids = jnp.arange(2 * SPAN + 1, dtype=jnp.int32)
    source_dom = dom_index - (offset_ids - SPAN)
    valid_source = (source_dom >= 0) & (source_dom < N_DOM)
    source = jnp.clip(source_dom, 0, N_DOM - 1)[:, None] * N_SUB + jnp.arange(N_SUB, dtype=jnp.int32)[None, :]
    taken_rows = blocks[source, :, :, offset_ids[:, None], sub_index, :]
    taken_rows = jnp.where(valid_source[:, None, None, None, None], taken_rows, jnp.zeros_like(taken_rows))
    return jnp.transpose(taken_rows, (2, 3, 0, 1, 4)).reshape(BASIS, QUANTS, POOL)


def reference(modal_state, star_matrices, face_normals, wave_speed, inverse_jacobian, stiffness, lift_minus, lift_plus, cluster, face_source, send_rows, send_counts):
    devices_all = jnp.arange(N_DOM * N_SUB, dtype=jnp.int32)
    intervals = ((0.0, half_step), (half_step, 2.0 * half_step))

    def local(operand, device):
        return lax.dynamic_slice_in_dim(operand, device * ELEM_DEV, ELEM_DEV, operand.ndim - 1)

    def opening(device):
        state_now = local(modal_state, device)
        star_local = local(star_matrices, device)
        early_int, late_int = integrals(state_now, star_local, stiffness, intervals)
        return state_now, star_local, early_int, late_int

    def section_one(device):
        early_int = opening(device)[2]
        return outgoing(early_int, send_rows[device, 0], send_counts[device, 0])

    first_blocks = lax.map(section_one, devices_all)

    def middle(device):
        state_now, star_local, early_int, late_int = opening(device)
        normal_local = local(face_normals, device)
        speed_local = local(wave_speed, device)
        jacobian_local = local(inverse_jacobian, device)
        faces_local = local(face_source, device)
        is_fine = local(cluster, device) == 0
        first_pool = pull(first_blocks, device)
        sources = neighbours(early_int, first_pool, faces_local)
        fine_mid = state_now + jacobian_local * update(early_int, sources, star_local, normal_local, speed_local, stiffness, lift_minus, lift_plus)
        fine_int = integrals(fine_mid, star_local, stiffness, ((0.0, half_step),))[0]
        fine_value = jnp.where(is_fine, fine_int, late_int)
        coarse_value = early_int + fine_value
        return state_now, star_local, normal_local, speed_local, jacobian_local, faces_local, is_fine, fine_mid, fine_int, fine_value, coarse_value

    def section_two(device):
        parts_now = middle(device)
        fine_value, coarse_value = parts_now[9], parts_now[10]
        return (outgoing(fine_value, send_rows[device, 0], send_counts[device, 0]), outgoing(coarse_value, send_rows[device, 1], send_counts[device, 1]))

    second_blocks, coarse_blocks = lax.map(section_two, devices_all)

    def section_three(device):
        state_now, star_local, normal_local, speed_local, jacobian_local, faces_local, is_fine, fine_mid, fine_int, fine_value, coarse_value = middle(device)
        second_pool = pull(second_blocks, device)
        coarse_pool = pull(coarse_blocks, device)
        fine_end = fine_mid + jacobian_local * update(fine_int, neighbours(fine_value, second_pool, faces_local), star_local, normal_local, speed_local, stiffness, lift_minus, lift_plus)
        coarse_end = state_now + jacobian_local * update(coarse_value, neighbours(coarse_value, coarse_pool, faces_local), star_local, normal_local, speed_local, stiffness, lift_minus, lift_plus)
        return jnp.where(is_fine, fine_end, coarse_end)

    new_state = lax.map(section_three, devices_all)
    return jnp.transpose(new_state, (1, 2, 0, 3)).reshape(BASIS, QUANTS, ELEMENTS)
```

```python
import functools
import math

import jax
import jax.numpy as jnp
from jax import lax
from jax.experimental import pallas as pl
from jax.experimental.pallas import tpu as pltpu
from jax.sharding import Mesh
from jax.sharding import PartitionSpec as P

B, BP, Q, E = 35, 40, 9, 128
W = Q * E
ROWS = 384
DEGREE = 4
SPAN = 2
NSUB = 4
NOFF = 2 * SPAN + 1
SLOTS = 4
DEST = 2 * NSUB
F32, BF16 = jnp.float32, jnp.bfloat16
VMEM_LIMIT = 60 * 1024 * 1024


def lanes(q):
    return slice(q * E, (q + 1) * E)


def hi_lo(x):
    hi = x.astype(BF16).astype(F32)
    return hi, x - hi


def stack_three(hi, lo):
    return jnp.concatenate([hi, lo, hi, jnp.zeros((8, E), F32)], axis=0).astype(BF16)


def matmul(a, b):
    return lax.dot_general(a, b, (((1,), (0,)), ((), ())), preferred_element_type=F32)


def rows_of(ref, index, row):
    return jnp.broadcast_to(ref[index + (slice(row, row + 1),)], (8, E))


def mix(src, star, group=3):
    for start in range(0, Q, group):
        qs = range(start, min(Q, start + group))
        totals = {q: [None] * 5 for q in qs}
        for p in range(Q):
            for d in range(3):
                tiles = [src[d * BP + 8 * i : d * BP + 8 * i + 8, lanes(p)] for i in range(5)]
                for q in qs:
                    factor = rows_of(star, (p, q), d)
                    for i in range(5):
                        term = tiles[i] * factor
                        totals[q][i] = term if totals[q][i] is None else totals[q][i] + term
        for q in qs:
            yield q, totals[q]


def fill_stack(dst, src):
    for q in range(Q):
        hi, lo = hi_lo(src[:, lanes(q)])
        dst[:, lanes(q)] = stack_three(hi, lo)


def place_matrix(scr, base, value):
    hi, lo = hi_lo(value)
    scr[base : base + B, 0:B] = hi
    scr[base : base + B, BP : BP + B] = hi
    scr[base : base + B, 2 * BP : 2 * BP + B] = lo


def fill_rows(dst, src):
    for q in range(Q):
        hi, lo = hi_lo(src[:, lanes(q)])
        dst[q * BP : (q + 1) * BP, 0:E] = hi
        dst[q * BP : (q + 1) * BP, E : 2 * E] = lo
    dst[Q * BP :, :] = jnp.zeros((ROWS - Q * BP, 2 * E), F32)


def predictor(stack, z, kmat, star, first, targets):
    for q in range(Q):
        tile = first[:, lanes(q)]
        for ref, coefs in targets:
            ref[:, lanes(q)] = coefs[0] * tile
    fill_stack(stack, first)

    def body(k, carry):
        z[...] = matmul(kmat[...], stack[...])
        scales = []
        for _, coefs in targets:
            scale = jnp.float32(coefs[DEGREE])
            for degree in range(DEGREE - 1, 0, -1):
                scale = jnp.where(k == degree, jnp.float32(coefs[degree]), scale)
            scales.append(scale)
        for q, tiles in mix(z, star):
            value = jnp.concatenate(tiles, axis=0)
            for (ref, _), scale in zip(targets, scales):
                ref[:, lanes(q)] = ref[:, lanes(q)] + scale * value
            hi, lo = hi_lo(value)
            stack[:, lanes(q)] = stack_three(hi, lo)
        return carry

    lax.fori_loop(1, DEGREE + 1, body, 0)


def taylor(lower, upper):
    return [(upper ** (k + 1) - lower ** (k + 1)) / math.factorial(k + 1) for k in range(DEGREE + 1)]


EARLY, LATE = taylor(0.0, 0.5), taylor(0.5, 1.0)


def one_hot_rows(dst, rows_s, counts_s, lists, which):
    lane = lax.broadcasted_iota(jnp.int32, (1, E), 1)
    for o in range(NOFF):
        for u in range(NSUB):
            for at, which_list in enumerate(lists):
                row = ((o * NSUB + u) * len(lists) + at) * SLOTS
                if which_list != which:
                    dst[row : row + SLOTS, :] = jnp.zeros((SLOTS, E), F32)
                    continue
                count = counts_s[0, which_list, u, o]
                for j in range(SLOTS):
                    index = jnp.where(j < count, rows_s[0, which_list, u, j, o], -1)
                    dst[row + j : row + j + 1, :] = jnp.where(lane == index, 1.0, 0.0)


def send_blocks(table, value, depth, outs):
    for block in range(NOFF * NSUB):
        table[block] = value[block * depth : (block + 1) * depth, :]
    table[NOFF * NSUB] = jnp.zeros((depth, ROWS), F32)
    core = lax.axis_index("core")
    toward = 1 - 2 * (lax.axis_index("chip") % 2)
    for hop, out in zip((0, toward, -toward), outs):
        for to_core in range(2):
            offset = 2 * hop + to_core - core + SPAN
            fits = (offset >= 0) & (offset < NOFF)
            for u in range(NSUB):
                block = jnp.where(fits, offset * NSUB + u, NOFF * NSUB)
                out[to_core * NSUB + u] = table[block]


def pick(one_hot, rows):
    both = jnp.concatenate([one_hot, one_hot], axis=1).astype(BF16)
    return lax.dot_general(both, rows, (((1,), (1,)), ((), ())), preferred_element_type=F32)


def first_kernel(state, star, stiffness, rows_s, counts_s, early, late, kmat, own, near, far, first, stack, z, mats, rows, one_hot, table):
    first[32:BP, :] = jnp.zeros((8, W), F32)
    for q in range(Q):
        first[0:B, lanes(q)] = state[q]
    mats[...] = jnp.zeros(mats.shape, F32)
    for d in range(3):
        place_matrix(mats, d * BP, -stiffness[d])
    kmat[...] = mats[...].astype(BF16)
    one_hot_rows(one_hot, rows_s, counts_s, (0,), 0)
    predictor(stack, z, kmat, star, first, ((early, EARLY), (late, LATE)))
    fill_rows(rows, early)
    send_blocks(table, pick(one_hot[...], rows[...].astype(BF16)), SLOTS, (own, near, far))


def own_part(field, minus, normals, out, stack, z):
    fill_stack(stack, field)
    z[...] = matmul(minus[...], stack[...])
    scale = [[-0.5 * rows_of(normals, (d,), f) for f in range(4)] for d in range(3)]
    for q in range(Q):
        for i in range(5):
            part = [z[(3 + f) * BP + 8 * i : (3 + f) * BP + 8 * i + 8, lanes(q)] for f in range(4)]
            for d in range(3):
                total = z[d * BP + 8 * i : d * BP + 8 * i + 8, lanes(q)]
                for f in range(4):
                    total = total + scale[d][f] * part[f]
                out[d * BP + 8 * i : d * BP + 8 * i + 8, lanes(q)] = total
            out[3 * BP + 8 * i : 3 * BP + 8 * i + 8, lanes(q)] = part[0] + part[1] + (part[2] + part[3])


def prepare_kernel(early, stiffness, lift_minus, lift_plus, normals, half, minus, plus, stack, z, mats):
    mats[...] = jnp.zeros(mats.shape, F32)
    for d in range(3):
        place_matrix(mats, d * BP, jnp.transpose(stiffness[d]))
    for f in range(4):
        place_matrix(mats, (3 + f) * BP, lift_minus[:, f, :])
        place_matrix(mats, (7 + f) * BP, lift_plus[:, f, :])
    minus[...] = mats[0 : 7 * BP].astype(BF16)
    plus[...] = mats[7 * BP :].astype(BF16)
    own_part(early, minus, normals, half, stack, z)


def half_kernel(field, minus, normals, half, stack, z):
    own_part(field, minus, normals, half, stack, z)


def pool_position(faces, depth, shift):
    row = faces - E
    offset, source_sub, slot = (row >> 4) - SPAN, (row >> 2) & 3, row & 3
    behind = lax.axis_index("core") - offset
    source_core, hop = behind & 1, behind >> 1
    toward = 1 - 2 * (lax.axis_index("chip") % 2)
    block = jnp.where(hop == 0, 0, jnp.where(hop == toward, 1, 2))
    return ((source_core * NSUB + source_sub) * 3 + block) * depth + slot + shift


def pool_columns(pool, pool_rows, pool_sem, received, depth, width):
    copy = pltpu.make_async_copy(received, pool, pool_sem)
    copy.start()
    copy.wait()
    for source in range(DEST):
        for block in range(3):
            at = (source * 3 + block) * depth
            pool_rows[at : at + depth, :] = pool[source, block]
    if width > 3 * DEST * depth:
        pool_rows[3 * DEST * depth :, :] = jnp.zeros((width - 3 * DEST * depth, ROWS), F32)
    return hi_lo(jnp.transpose(pool_rows[...]))


def face_part(sources, hot, plus, half, normals, stack, part, x, speed_term, gathered):
    gathered[...] = matmul(sources[...], hot[...])
    for f in range(4):
        for q in range(Q):
            hi = gathered[q * BP : (q + 1) * BP, lanes(f)]
            lo = gathered[ROWS + q * BP : ROWS + (q + 1) * BP, lanes(f)]
            stack[:, lanes(q)] = stack_three(hi, lo)
        part[f * BP : (f + 1) * BP, :] = matmul(plus[f * BP : (f + 1) * BP, :], stack[...])
    scale = [[-0.5 * rows_of(normals, (d,), f) for f in range(4)] for d in range(3)]
    for q in range(Q):
        for i in range(5):
            tiles = [part[f * BP + 8 * i : f * BP + 8 * i + 8, lanes(q)] for f in range(4)]
            for d in range(3):
                total = half[d * BP + 8 * i : d * BP + 8 * i + 8, lanes(q)]
                for f in range(4):
                    total = total + scale[d][f] * tiles[f]
                x[d * BP + 8 * i : d * BP + 8 * i + 8, lanes(q)] = total
            own = half[3 * BP + 8 * i : 3 * BP + 8 * i + 8, lanes(q)]
            speed_term[8 * i : 8 * i + 8, lanes(q)] = own - (tiles[0] + tiles[1] + (tiles[2] + tiles[3]))


def hot_columns(hot, positions):
    row = lax.broadcasted_iota(jnp.int32, (hot.shape[0], E), 0)
    for f in range(4):
        hot[:, lanes(f)] = jnp.where(row == positions[f : f + 1, :], 1.0, 0.0).astype(BF16)


def wide(ref):
    return jnp.broadcast_to(ref[...], (8, E))


def middle_kernel(
    state, star, early, late, half, normals, speed, jacobian, cluster, faces, kmat, plus, rows_s, counts_s, received,
    base, fine, integral, own, near, far,
    stack, z, part, x, term, sources, hot, gathered, pool, pool_rows, rows, rows_two, one_hot, one_hot_two, table, mid, fine_int, coarse, pool_sem,
):
    hot_columns(hot, jnp.where(faces[...] < E, faces[...], E + pool_position(faces[...], SLOTS, 0)))
    one_hot_rows(one_hot, rows_s, counts_s, (0, 1), 0)
    one_hot_rows(one_hot_two, rows_s, counts_s, (0, 1), 1)
    fill_rows(rows, early)
    hi, lo = pool_columns(pool, pool_rows, pool_sem, received, SLOTS, E)
    sources[0:ROWS, 0:E] = rows[:, 0:E].astype(BF16)
    sources[ROWS:, 0:E] = rows[:, E:].astype(BF16)
    sources[0:ROWS, E:] = hi.astype(BF16)
    sources[ROWS:, E:] = lo.astype(BF16)
    face_part(sources, hot, plus, half, normals, stack, part, x, term, gathered)
    is_fine = wide(cluster) == 0
    half_speed, factor = 0.5 * wide(speed), wide(jacobian)
    for q, tiles in mix(x, star):
        for i in range(5):
            size = min(8, B - 8 * i)
            at = slice(8 * i, 8 * i + 8)
            start = state[q, 8 * i : 8 * i + size, :]
            if size < 8:
                start = jnp.concatenate([start, jnp.zeros((8 - size, E), F32)], axis=0)
            value = start + factor * (tiles[i] - half_speed * term[at, lanes(q)])
            mid[at, lanes(q)] = value
            base[at, lanes(q)] = jnp.where(is_fine, value, start)
    predictor(stack, z, kmat, star, mid, ((fine_int, EARLY),))
    for q in range(Q):
        for i in range(5):
            at = slice(8 * i, 8 * i + 8)
            value = fine_int[at, lanes(q)]
            fine_value = jnp.where(is_fine, value, late[at, lanes(q)])
            coarse_value = early[at, lanes(q)] + fine_value
            fine[at, lanes(q)] = fine_value
            coarse[at, lanes(q)] = coarse_value
            integral[at, lanes(q)] = jnp.where(is_fine, value, coarse_value)
    fill_rows(rows, fine)
    fill_rows(rows_two, coarse)
    value = pick(one_hot[...], rows[...].astype(BF16)) + pick(one_hot_two[...], rows_two[...].astype(BF16))
    send_blocks(table, value, 2 * SLOTS, (own, near, far))


def last_kernel(
    base, star, early, fine, half, normals, speed, jacobian, cluster, faces, plus, received, out,
    stack, part, x, term, sources, hot, gathered, pool, pool_rows, rows, rows_two, coarse, pool_sem,
):
    is_coarse = cluster[...] != 0
    place = jnp.where(is_coarse, SLOTS, 0)
    local = faces[...] + jnp.where(is_coarse, E, 0)
    hot_columns(hot, jnp.where(faces[...] < E, local, 2 * E + pool_position(faces[...], 2 * SLOTS, place)))
    for q in range(Q):
        coarse[:, lanes(q)] = early[:, lanes(q)] + fine[:, lanes(q)]
    fill_rows(rows, fine)
    fill_rows(rows_two, coarse)
    hi, lo = pool_columns(pool, pool_rows, pool_sem, received, 2 * SLOTS, 2 * E)
    for at, ref in ((0, rows), (E, rows_two)):
        sources[0:ROWS, at : at + E] = ref[:, 0:E].astype(BF16)
        sources[ROWS:, at : at + E] = ref[:, E:].astype(BF16)
    sources[0:ROWS, 2 * E :] = hi.astype(BF16)
    sources[ROWS:, 2 * E :] = lo.astype(BF16)
    face_part(sources, hot, plus, half, normals, stack, part, x, term, gathered)
    half_speed, factor = 0.5 * wide(speed), wide(jacobian)
    for q, tiles in mix(x, star):
        for i in range(5):
            at = slice(8 * i, 8 * i + 8)
            value = base[at, lanes(q)] + factor * (tiles[i] - half_speed * term[at, lanes(q)])
            size = min(8, B - 8 * i)
            out[q, 8 * i : 8 * i + size, :] = value[0:size]


def call(kernel, name, operands, outs, scratch, flops):
    return pl.pallas_call(
        kernel,
        name=name,
        in_specs=[pl.BlockSpec(memory_space=space) for _, space in operands],
        out_specs=[pl.BlockSpec(memory_space=pltpu.VMEM)] * len(outs),
        out_shape=[jax.ShapeDtypeStruct(shape, dtype) for shape, dtype in outs],
        scratch_shapes=[pltpu.SemaphoreType.DMA if s is None else pltpu.VMEM(*s) for s in scratch],
        compiler_params=pltpu.CompilerParams(vmem_limit_bytes=VMEM_LIMIT),
        cost_estimate=pl.CostEstimate(flops=flops, bytes_accessed=2_000_000, transcendentals=0),
    )(*[array for array, _ in operands])


def exchange(own, near, far):
    chips = lax.axis_size("chip")
    with_first = [(i, i ^ 1) for i in range(chips)]
    with_second = [(i, i + 1 if i % 2 else i - 1) for i in range(1, chips - 1)]
    far = lax.ppermute(far, "chip", with_second)
    near = lax.ppermute(near, "chip", with_first)
    blocks = jnp.stack([own, near, far], axis=1)
    return lax.all_to_all(blocks, ("core", "sub"), 0, 0, tiled=True)


def per_device(
    modal_state,
    star_matrices,
    face_normals,
    wave_speed,
    inverse_jacobian,
    stiffness,
    lift_minus,
    lift_plus,
    cluster,
    face_source,
    send_rows,
    send_counts,
):
    V, S, A = pltpu.VMEM, pltpu.SMEM, pl.ANY
    state = (jnp.transpose(modal_state, (1, 0, 2)), V)
    star = (jnp.transpose(star_matrices, (1, 2, 0, 3)), V)
    rows_s = (jnp.transpose(send_rows, (0, 1, 3, 4, 2)), S)
    counts_s = (jnp.transpose(send_counts, (0, 1, 3, 2)), S)
    speed, jacobian, kind = ((v.reshape(1, E), V) for v in (wave_speed, inverse_jacobian, cluster))
    normals, faces = (face_normals, V), (face_source, V)
    field = ((BP, W), F32)
    stack, z = ((E, W), BF16), ((3 * BP, W), F32)
    rows = ((ROWS, 2 * E), F32)

    def blocks(depth):
        return [((DEST, depth, ROWS), F32)] * 3

    def table(depth):
        return ((NOFF * NSUB + 1, depth, ROWS), F32)

    early, late, kmat, *parts = call(
        first_kernel,
        "first",
        [state, star, (stiffness, V), rows_s, counts_s],
        [field, field, ((3 * BP, E), BF16)] + blocks(SLOTS),
        [field, stack, z, ((3 * BP, E), F32), rows, ((NOFF * NSUB * SLOTS, E), F32), table(SLOTS)],
        10**9,
    )
    early, late, kmat = (early, V), (late, V), (kmat, V)
    received = exchange(*parts)
    half, minus, plus = call(
        prepare_kernel,
        "prepare",
        [early, (stiffness, V), (jnp.transpose(lift_minus, (1, 0, 2)), V), (jnp.transpose(lift_plus, (1, 0, 2)), V), normals],
        [((4 * BP, W), F32), ((7 * BP, E), BF16), ((4 * BP, E), BF16)],
        [stack, ((7 * BP, W), F32), ((11 * BP, E), F32)],
        10**9,
    )
    minus, plus = (minus, V), (plus, V)
    base, fine, integral, *parts = call(
        middle_kernel,
        "middle",
        [state, star, early, late, (half, V), normals, speed, jacobian, kind, faces, kmat, plus, rows_s, counts_s, (received, A)],
        [field, field, field] + blocks(2 * SLOTS),
        [
            stack, z, ((4 * BP, W), F32), z, field, ((2 * ROWS, 2 * E), BF16), ((2 * E, 4 * E), BF16), ((2 * ROWS, 4 * E), F32),
            ((DEST, 3, SLOTS, ROWS), F32), ((E, ROWS), F32), rows, rows, ((NOFF * NSUB * 2 * SLOTS, E), F32),
            ((NOFF * NSUB * 2 * SLOTS, E), F32), table(2 * SLOTS), field, field, field, None,
        ],
        2 * 10**9,
    )
    received = exchange(*parts)
    half = call(
        half_kernel,
        "half",
        [(integral, V), minus, normals],
        [((4 * BP, W), F32)],
        [stack, ((7 * BP, W), F32)],
        10**9,
    )[0]
    out = call(
        last_kernel,
        "last",
        [(base, V), star, early, (fine, V), (half, V), normals, speed, jacobian, kind, faces, plus, (received, A)],
        [((Q, B, E), F32)],
        [
            stack, ((4 * BP, W), F32), z, field, ((2 * ROWS, 4 * E), BF16), ((4 * E, 4 * E), BF16), ((2 * ROWS, 4 * E), F32),
            ((DEST, 3, 2 * SLOTS, ROWS), F32), ((2 * E, ROWS), F32), rows, rows, field, None,
        ],
        2 * 10**9,
    )[0]
    return jnp.transpose(out, (1, 0, 2))


def solution(mesh):
    chips = mesh.devices.size // (2 * NSUB)
    fine_mesh = Mesh(mesh.devices.reshape(chips, 2, NSUB), ("chip", "core", "sub"))
    every = ("chip", "core", "sub")
    placed = (
        P(None, None, every),
        P(None, None, None, every),
        P(None, None, every),
        P(every),
        P(every),
        P(),
        P(),
        P(),
        P(every),
        P(None, every),
        P(every, None, None, None, None),
        P(every, None, None, None),
    )
    return jax.shard_map(
        per_device,
        mesh=fine_mesh,
        in_specs=placed,
        out_specs=P(None, None, every),
        check_vma=False,
    )
```
